32 devices in a mesh: dp: 8 (over y, x, core), tensor: 4 (over z).
Axes of the slice: x: 2, y: 2, z: 4, core: 2. Of those that a mesh axis runs over, the one named last changes fastest.
Arguments:
- tokens: bfloat16 [8192, 2048], P(('dp', 'tensor')), may hold values from -6 to 6
- lengths: int32 [8, 8], P('dp'), may hold values from 0 to 1024, as said below
- qkv_weight: bfloat16 [2048, 6144], P(None, 'tensor'), may hold values from -0.1875 to 0.1875
- qkv_bias: bfloat16 [6144], P('tensor'), may hold values from -3 to 3
- dense_weight: bfloat16 [2048, 2048], P('tensor'), may hold values from -0.5 to 0.5
- dense_bias: bfloat16 [2048], replicated, may hold values from -3 to 3
- up_weight: bfloat16 [2048, 8192], P(None, 'tensor'), may hold values from -0.125 to 0.125
- up_bias: bfloat16 [8192], P('tensor'), may hold values from -3 to 3
- down_weight: bfloat16 [8192, 2048], P('tensor'), may hold values from -0.125 to 0.125
- down_bias: bfloat16 [2048], replicated, may hold values from -3 to 3
- gain_attn: bfloat16 [2048], replicated, may hold values from 0.5 to 1.5
- shift_attn: bfloat16 [2048], replicated, may hold values from -3 to 3
- gain_mlp: bfloat16 [2048], replicated, may hold values from 0.5 to 1.5
- shift_mlp: bfloat16 [2048], replicated, may hold values from -3 to 3
- out_grad: bfloat16 [8192, 2048], P(('dp', 'tensor')), may hold values from -6 to 6
Outputs:
- output: bfloat16 [8192, 2048], P(('dp', 'tensor'))
- grad_tokens: float32 [8192, 2048], P(('dp', 'tensor'))
- grad_qkv_weight: float32 [2048, 6144], P(None, 'tensor')
- grad_qkv_bias: float32 [6144], P('tensor')
- grad_dense_weight: float32 [2048, 2048], P('tensor')
- grad_dense_bias: float32 [2048], replicated
- grad_up_weight: float32 [2048, 8192], P(None, 'tensor')
- grad_up_bias: float32 [8192], P('tensor')
- grad_down_weight: float32 [8192, 2048], P('tensor')
- grad_down_bias: float32 [2048], replicated
- grad_gain_attn: float32 [2048], replicated
- grad_shift_attn: float32 [2048], replicated
- grad_gain_mlp: float32 [2048], replicated
- grad_shift_mlp: float32 [2048], replicated
The draws below stay inside these ranges and needn't reach their ends.
Inputs may be any that keep to these rules, and one draw needn't show every extreme that they name: Each row of lengths sums to 1024. In half of the rows slot 0 holds a sequence of 1024 tokens and the next 7 slots are 0. Every other pair of slots 2 b, 2 b + 1 covers the group's tokens b * 256 to (b + 1) * 256 - 1, either as one sequence of 256 tokens and a 0, or as two sequences of 64 to 192 tokens.
All inputs are finite; a program needn't handle non-finite values.
Results may differ from the reference program's by a relative error of at most 0.015.
The reference program's roundings to bfloat16 on the way count: a program that leaves them out, or rounds other values in their place, can miss the bound.
Values may be sent and summed in bfloat16 or wider, within the bound.
No kernel may reach another device: no remote copies, remote signals or barrier semaphores. Data moves between devices by JAX's collectives and lax.ppermute only.
A program may use at most 256 MiB of HBM per device.

```python
import jax
import jax.numpy as jnp
from jax import lax

D = 2048
HEADS = 16
HEAD_DIM = 128
ROT = 32
FF = 8192
LONG = 1024
BLOCK = 256
QBLK = 512
GROUP = 1024
TOKENS = 8192
N_DP = 8


def draw_lengths(key, part):
    block_count = GROUP // BLOCK
    long_blocks = LONG // BLOCK
    pick_key, split_key, cut_key = jax.random.split(key, 3)
    order = jax.random.permutation(pick_key, N_DP)
    is_long = order < N_DP // 2
    splits = jax.random.randint(split_key, (N_DP, block_count), 0, 2)
    cuts = jax.random.randint(cut_key, (N_DP, block_count), BLOCK // 4, 3 * BLOCK // 4 + 1)
    first_part = jnp.where(splits == 1, cuts, BLOCK)
    second_part = BLOCK - first_part
    block_ids = jnp.arange(block_count)[None, :]
    inside = (block_ids < long_blocks) & is_long[:, None]
    first_part = jnp.where(inside, 0, first_part)
    second_part = jnp.where(inside, 0, second_part)
    leading = (block_ids == 0) & is_long[:, None]
    first_part = jnp.where(leading, LONG, first_part)
    paired = jnp.stack([first_part, second_part], axis=2)
    return paired.reshape(N_DP, 2 * block_count).astype(jnp.int32)


def block_levels(stream_key, extent, shards, smallest, top_value):
    gain = 1.0
    for axis_at, blocks in shards:
        heights = jax.random.uniform(jax.random.fold_in(jax.random.fold_in(stream_key, 6), axis_at), (blocks,), jnp.float32, smallest / len(shards), top_value / len(shards))
        gain = gain * jnp.repeat(jnp.exp(heights), extent[axis_at] // blocks).reshape((-1,) + (1,) * (len(extent) - 1 - axis_at))
    return gain


def noise(own_key, extent, spread, bound, cuts=(), kind=jnp.bfloat16):
    values = jax.random.normal(own_key, extent, jnp.float32) * spread
    if len(cuts) > 0:
        values = block_levels(own_key, extent, cuts, -0.22, 0.18) * values
    return jnp.clip(values, min=-bound, max=bound).astype(kind)


def setup_inputs(seed: int = 0) -> dict:
    streams_of = jax.random.split(jax.random.key(seed), 16)
    tokens = noise(streams_of[0], (TOKENS, D), 1.0, 6.0, ((0, 32),))
    lengths = draw_lengths(jax.random.fold_in(streams_of[15], 71), 0)
    qkv_weight = noise(streams_of[2], (D, 3 * D), (D // 2) ** -0.5, 0.1875, ((1, 4),))
    qkv_bias = noise(streams_of[3], (3 * D,), 0.5, 3.0, ((0, 4),))
    dense_weight = noise(streams_of[4], (D, D), (D // 16) ** -0.5, 0.5, ((0, 4),))
    dense_bias = noise(streams_of[5], (D,), 0.5, 3.0)
    up_weight = noise(streams_of[6], (D, FF), D ** -0.5, 0.125, ((1, 4),))
    up_bias = noise(streams_of[7], (FF,), 0.5, 3.0, ((0, 4),))
    down_weight = noise(streams_of[8], (FF, D), (FF // 4) ** -0.5, 0.125, ((0, 4),))
    down_bias = noise(streams_of[9], (D,), 0.5, 3.0)
    gain_attn = jnp.clip(1.0 + 0.1 * jax.random.normal(streams_of[10], (D,), jnp.float32), 0.5, 1.5).astype(jnp.bfloat16)
    shift_attn = noise(streams_of[11], (D,), 0.5, 3.0)
    gain_mlp = jnp.clip(1.0 + 0.1 * jax.random.normal(streams_of[12], (D,), jnp.float32), 0.5, 1.5).astype(jnp.bfloat16)
    shift_mlp = noise(streams_of[13], (D,), 0.5, 3.0)
    out_grad = noise(streams_of[14], (TOKENS, D), 1.0, 6.0, ((0, 32),))
    return dict(tokens=tokens, lengths=lengths, qkv_weight=qkv_weight, qkv_bias=qkv_bias, dense_weight=dense_weight, dense_bias=dense_bias, up_weight=up_weight, up_bias=up_bias, down_weight=down_weight, down_bias=down_bias, gain_attn=gain_attn, shift_attn=shift_attn, gain_mlp=gain_mlp, shift_mlp=shift_mlp, out_grad=out_grad)


EPSILON = 1e-05
MASKED = -1e+30

@jax.custom_vjp
def low(v):
    return lax.optimization_barrier(v.astype(jnp.bfloat16)).astype(jnp.float32)

@jax.custom_vjp
def low_back(v):
    return v

def low_keep(v):
    return (low(v), None)

def low_pass(kept, grad):
    return (grad,)

def back_keep(v):
    return (v, None)

def back_low(kept, grad):
    return (low(grad),)
low.defvjp(low_keep, low_pass)
low_back.defvjp(back_keep, back_low)

def product(left_side, right_side):
    return jnp.dot(left_side, right_side, precision=lax.Precision.HIGHEST, preferred_element_type=jnp.float32)

def layout(lengths):
    seq_ends = jnp.cumsum(lengths).astype(jnp.int32)
    row_ids = jnp.arange(GROUP, dtype=jnp.int32)
    passed = (seq_ends[None, :] <= row_ids[:, None]).astype(jnp.int32)
    segment = lax.optimization_barrier(jnp.sum(passed, axis=1)).astype(jnp.int32)
    position = (row_ids - lax.optimization_barrier(jnp.sum(passed * lengths[None, :], axis=1))).astype(jnp.int32)
    return (segment, position)

def rotary_tables(position):
    exponents = jnp.arange(0, ROT, 2, dtype=jnp.float32) / ROT
    inv_freq = 1.0 / 10000.0 ** exponents
    angles = position.astype(jnp.float32)[:, None] * inv_freq[None, :]
    angles = jnp.concatenate([angles, angles], axis=1)
    return (jnp.cos(angles)[:, None, :], jnp.sin(angles)[:, None, :])

def rotate(head_part, cosine_table, sine_table):
    half_rot = ROT // 2
    leading = head_part[..., :ROT]
    turned = jnp.concatenate([-leading[..., half_rot:], leading[..., :half_rot]], axis=-1)
    return jnp.concatenate([leading * cosine_table + turned * sine_table, head_part[..., ROT:]], axis=-1)

def attention(query_vectors, key_vectors, value_vectors, segment):
    block_rows = min(QBLK, GROUP)
    key_rows = jnp.arange(GROUP, dtype=jnp.int32)
    score_scale = HEAD_DIM ** (-0.5)

    def one_block(block_start):
        query_block = lax.dynamic_slice_in_dim(query_vectors, block_start, block_rows, 0)
        query_rows = block_start + jnp.arange(block_rows, dtype=jnp.int32)
        query_segment = lax.dynamic_slice_in_dim(segment, block_start, block_rows, 0)
        allowed = (query_segment[:, None] == segment[None, :]) & (key_rows[None, :] <= query_rows[:, None])
        scores = jnp.einsum('qhd,khd->hqk', query_block, key_vectors, precision=lax.Precision.HIGHEST) * score_scale
        scores = low_back(jnp.where(allowed[None], scores, MASKED))
        weights = low(jax.nn.softmax(scores, axis=-1))
        return jnp.einsum('hqk,khd->qhd', weights, value_vectors, precision=lax.Precision.HIGHEST)
    block_starts = jnp.arange(GROUP // block_rows, dtype=jnp.int32) * block_rows
    blocks = lax.map(jax.checkpoint(one_block), block_starts)
    return blocks.reshape(GROUP, HEADS, HEAD_DIM)

def group_forward(params, group_rows, segment, position):
    qkv_weight, qkv_bias, dense_weight, dense_bias, up_weight, up_bias, down_weight, down_bias, gain_attn, shift_attn, gain_mlp, shift_mlp = params
    average = lax.optimization_barrier(jnp.mean(group_rows, axis=1, keepdims=True))
    centred = group_rows - average
    scaled = centred * lax.rsqrt(lax.optimization_barrier(jnp.mean(centred * centred, axis=1, keepdims=True)) + EPSILON)
    normed_attn = low(scaled * gain_attn + shift_attn)
    normed_mlp = low(scaled * gain_mlp + shift_mlp)
    mixed_proj = low_back(product(normed_attn, qkv_weight) + qkv_bias).reshape(GROUP, HEADS, 3, HEAD_DIM)
    cosine_table, sine_table = rotary_tables(position)
    query_vectors = low(rotate(mixed_proj[:, :, 0], cosine_table, sine_table))
    key_vectors = low(rotate(mixed_proj[:, :, 1], cosine_table, sine_table))
    value_vectors = low(mixed_proj[:, :, 2])
    context = low_back(low(attention(query_vectors, key_vectors, value_vectors, segment))).reshape(GROUP, D)
    hidden = low_back(product(normed_mlp, up_weight) + up_bias)
    active = low(jax.nn.gelu(hidden, approximate=False))
    return group_rows + product(context, dense_weight) + dense_bias + product(active, down_weight) + down_bias

def reference(tokens, lengths, qkv_weight, qkv_bias, dense_weight, dense_bias, up_weight, up_bias, down_weight, down_bias, gain_attn, shift_attn, gain_mlp, shift_mlp, out_grad):
    params = tuple((array.astype(jnp.float32) for array in (qkv_weight, qkv_bias, dense_weight, dense_bias, up_weight, up_bias, down_weight, down_bias, gain_attn, shift_attn, gain_mlp, shift_mlp)))
    rows_all = tokens.astype(jnp.float32).reshape(N_DP, GROUP, D)
    cot_all = out_grad.astype(jnp.float32).reshape(N_DP, GROUP, D)

    def one_group(totals, group_item):
        group_rows, group_lengths, cotangent = group_item
        segment, position = layout(group_lengths)

        def forward(weight_set, inputs):
            return group_forward(weight_set, inputs, segment, position)
        result, pullback = jax.vjp(forward, params, group_rows)
        grad_params, grad_rows = pullback(cotangent)
        totals = tuple((first_term + second_term for first_term, second_term in zip(totals, grad_params)))
        return (totals, (result.astype(jnp.bfloat16), grad_rows))
    zero_grads = tuple((jnp.zeros_like(array) for array in params))
    totals, (outputs, grad_rows) = lax.scan(one_group, zero_grads, (rows_all, lengths, cot_all))
    return (outputs.reshape(TOKENS, D), grad_rows.reshape(TOKENS, D), totals[0], totals[1], totals[2], totals[3], totals[4], totals[5], totals[6], totals[7], totals[8], totals[9], totals[10], totals[11])
```

```python
import jax
import jax.numpy as jnp
from jax import lax
from jax.experimental import pallas as pl
from jax.experimental.pallas import tpu as pltpu
from jax.sharding import PartitionSpec as P

HEAD_DIM = 128
ROT = 32
EPSILON = 1e-05
MASKED = -1e30
BF16 = jnp.bfloat16
F32 = jnp.float32


def standardize(row_block):
    average = jnp.mean(row_block, axis=1, keepdims=True)
    centred = row_block - average
    inverse = lax.rsqrt(jnp.mean(centred * centred, axis=1, keepdims=True) + EPSILON)
    return (centred * inverse, inverse)


def layout(lengths, group_size):
    seq_ends = jnp.cumsum(lengths)
    row_ids = jnp.arange(group_size, dtype=jnp.int32)
    passed = (seq_ends[None, :] <= row_ids[:, None]).astype(jnp.int32)
    first_row = jnp.sum(passed * lengths[None, :], axis=1)
    return (first_row, row_ids - first_row)


def rotary_tables(position):
    exponents = jnp.arange(0, ROT, 2, dtype=F32) / ROT
    inv_freq = 1.0 / 10000.0**exponents
    angles = position.astype(F32)[:, None] * inv_freq[None, :]
    cosine, sine = jnp.cos(angles), jnp.sin(angles)
    rows, half = angles.shape
    keep = jnp.concatenate([cosine, cosine, jnp.ones((rows, HEAD_DIM - ROT), F32)], axis=1)
    low = jnp.concatenate([-sine, jnp.zeros((rows, HEAD_DIM - half), F32)], axis=1)
    high = jnp.concatenate(
        [jnp.zeros((rows, half), F32), sine, jnp.zeros((rows, HEAD_DIM - ROT), F32)], axis=1
    )
    return (keep, low, high)


def turn(u, keep, low, high):
    return (
        u * keep
        + pltpu.roll(u, HEAD_DIM - ROT // 2, 1) * low
        + pltpu.roll(u, ROT // 2, 1) * high
    )


def turn_back(u, keep, low, high):
    return (
        u * keep
        - pltpu.roll(u, HEAD_DIM - ROT // 2, 1) * low
        - pltpu.roll(u, ROT // 2, 1) * high
    )


def dot_nt(a, b):
    return lax.dot_general(a, b, (((1,), (1,)), ((), ())), preferred_element_type=F32)


def dot_tn(a, b):
    return lax.dot_general(a, b, (((0,), (0,)), ((), ())), preferred_element_type=F32)


def dot_nn(a, b):
    return jnp.dot(a, b, preferred_element_type=F32)


def attend_kernel(blocks, place_ref, mixed_ref, keep_ref, low_ref, high_ref, first_ref, qkv_ref, context_ref):
    rows = mixed_ref.shape[0] // blocks
    scale = HEAD_DIM ** (-0.5)

    def slot(i):
        return pl.ds(pl.multiple_of(lax.rem(place_ref[0] - i + blocks, blocks) * rows, rows), rows)

    for i in range(blocks):
        here = slice(i * rows, (i + 1) * rows)
        tables = (keep_ref[here, :], low_ref[here, :], high_ref[here, :])
        there = slot(i)
        qkv_ref[here, 0:128] = turn(mixed_ref[there, 0:128], *tables).astype(BF16)
        qkv_ref[here, 128:256] = turn(mixed_ref[there, 128:256], *tables).astype(BF16)
        qkv_ref[here, 256:384] = mixed_ref[there, 256:384].astype(BF16)
    for i in range(blocks):
        count = (i + 1) * rows
        query = qkv_ref[i * rows : count, 0:128]
        scores = dot_nt(query, qkv_ref[0:count, 128:256]) * scale
        key_at = lax.broadcasted_iota(jnp.int32, scores.shape, 1)
        query_at = lax.broadcasted_iota(jnp.int32, scores.shape, 0) + i * rows
        seen = (key_at >= first_ref[i * rows : count, :]) & (key_at <= query_at)
        scores = jnp.where(seen, scores, MASKED)
        top = jnp.max(scores, axis=1, keepdims=True)
        raised = jnp.exp(scores - top)
        total = jnp.sum(raised, axis=1, keepdims=True)
        weights = (raised * (1.0 / total)).astype(BF16)
        context_ref[slot(i), :] = dot_nn(weights, qkv_ref[0:count, 256:384]).astype(BF16)


def attend(mixed, tables, first_row, place, blocks):
    group, width = mixed.shape
    heads = width // (3 * HEAD_DIM)
    whole = lambda h, p: (0, 0)
    by_head = lambda h, p: (0, h)
    table = pl.BlockSpec((group, HEAD_DIM), whole)
    return pl.pallas_call(
        lambda *refs: attend_kernel(blocks, *refs),
        out_shape=(
            jax.ShapeDtypeStruct((group, width), BF16),
            jax.ShapeDtypeStruct((group, heads * HEAD_DIM), BF16),
        ),
        grid_spec=pltpu.PrefetchScalarGridSpec(
            num_scalar_prefetch=1,
            grid=(heads,),
            in_specs=[
                pl.BlockSpec((group, 3 * HEAD_DIM), by_head),
                table,
                table,
                table,
                pl.BlockSpec((group, 1), whole),
            ],
            out_specs=(
                pl.BlockSpec((group, 3 * HEAD_DIM), by_head),
                pl.BlockSpec((group, HEAD_DIM), by_head),
            ),
        ),
        compiler_params=pltpu.CompilerParams(dimension_semantics=("arbitrary",)),
        name="attend",
    )(place, mixed, *tables, first_row[:, None])


def attend_back_kernel(
    blocks,
    place_ref,
    qkv_ref,
    grad_ref,
    keep_ref,
    low_ref,
    high_ref,
    first_ref,
    mixed_ref,
    sums_ref,
    keys_ref,
    values_ref,
):
    rows = qkv_ref.shape[0] // blocks
    scale = HEAD_DIM ** (-0.5)

    def slot(i):
        return pl.ds(pl.multiple_of(lax.rem(place_ref[0] - i + blocks, blocks) * rows, rows), rows)

    def tables(i):
        here = slice(i * rows, (i + 1) * rows)
        return (keep_ref[here, :], low_ref[here, :], high_ref[here, :])

    query_sum = jnp.zeros((1, HEAD_DIM), F32)
    key_sum = jnp.zeros((1, HEAD_DIM), F32)
    value_sum = jnp.zeros((1, HEAD_DIM), F32)
    for i in reversed(range(blocks)):
        count = (i + 1) * rows
        query = qkv_ref[i * rows : count, 0:128]
        keys = qkv_ref[0:count, 128:256]
        grad = grad_ref[slot(i), :]
        scores = dot_nt(keys, query) * scale
        key_at = lax.broadcasted_iota(jnp.int32, scores.shape, 0)
        query_at = lax.broadcasted_iota(jnp.int32, scores.shape, 1) + i * rows
        seen = (key_at >= first_ref[:, i * rows : count]) & (key_at <= query_at)
        scores = jnp.where(seen, scores, MASKED)
        top = jnp.max(scores, axis=0, keepdims=True)
        raised = jnp.exp(scores - top)
        total = jnp.sum(raised, axis=0, keepdims=True)
        probs = raised * (1.0 / total)
        grad_values = dot_nn(probs.astype(BF16), grad)
        grad_probs = dot_nt(qkv_ref[0:count, 256:384], grad)
        spread = jnp.sum(probs * grad_probs, axis=0, keepdims=True)
        grad_scores = (probs * (grad_probs - spread)).astype(BF16)
        grad_keys = dot_nn(grad_scores, query)
        if i == blocks - 1:
            values_ref[...] = grad_values
            keys_ref[...] = grad_keys
        else:
            values_ref[0:count, :] += grad_values
            keys_ref[0:count, :] += grad_keys
        grad_query = turn_back(dot_tn(grad_scores, keys) * scale, *tables(i)).astype(BF16)
        mixed_ref[slot(i), 0:128] = grad_query
        query_sum += jnp.sum(grad_query.astype(F32), axis=0, keepdims=True)
        here = slice(i * rows, count)
        if i == 0:
            for j in range(blocks):
                here = slice(j * rows, (j + 1) * rows)
                grad_key = turn_back(keys_ref[here, :] * scale, *tables(j)).astype(BF16)
                grad_value = values_ref[here, :].astype(BF16)
                mixed_ref[slot(j), 128:256] = grad_key
                mixed_ref[slot(j), 256:384] = grad_value
                key_sum += jnp.sum(grad_key.astype(F32), axis=0, keepdims=True)
                value_sum += jnp.sum(grad_value.astype(F32), axis=0, keepdims=True)
    sums_ref[:, 0:128] = jnp.broadcast_to(query_sum, (8, HEAD_DIM))
    sums_ref[:, 128:256] = jnp.broadcast_to(key_sum, (8, HEAD_DIM))
    sums_ref[:, 256:384] = jnp.broadcast_to(value_sum, (8, HEAD_DIM))


def attend_back(qkv, grad_context, tables, first_row, place, blocks):
    group, width = qkv.shape
    heads = width // (3 * HEAD_DIM)
    whole = lambda h, p: (0, 0)
    by_head = lambda h, p: (0, h)
    table = pl.BlockSpec((group, HEAD_DIM), whole)
    mixed, sums = pl.pallas_call(
        lambda *refs: attend_back_kernel(blocks, *refs),
        out_shape=(
            jax.ShapeDtypeStruct((group, width), BF16),
            jax.ShapeDtypeStruct((8, width), F32),
        ),
        grid_spec=pltpu.PrefetchScalarGridSpec(
            num_scalar_prefetch=1,
            grid=(heads,),
            in_specs=[
                pl.BlockSpec((group, 3 * HEAD_DIM), by_head),
                pl.BlockSpec((group, HEAD_DIM), by_head),
                table,
                table,
                table,
                pl.BlockSpec((1, group), whole),
            ],
            out_specs=(
                pl.BlockSpec((group, 3 * HEAD_DIM), by_head),
                pl.BlockSpec((8, 3 * HEAD_DIM), by_head),
            ),
            scratch_shapes=[pltpu.VMEM((group, HEAD_DIM), F32)] * 2,
        ),
        compiler_params=pltpu.CompilerParams(dimension_semantics=("arbitrary",)),
        name="attend_back",
    )(place, qkv, grad_context, *tables, first_row[None, :])
    return (mixed, sums[0])


def after(value, *earlier):
    return lax.optimization_barrier((value, *earlier))[0]


def line_gather(own, size):
    ups, downs = [own], [own]
    for step in range(1, size):
        ups.append(
            lax.ppermute(ups[-1], "tensor", [(i, i + 1) for i in range(step - 1, size - 1)])
        )
        downs.append(
            lax.ppermute(downs[-1], "tensor", [(i, i - 1) for i in range(1, size - step + 1)])
        )
    return [own] + [ups[k] + downs[size - k] for k in range(1, size)]


def line_scatter(partial, size):
    rows = partial.shape[0] // size

    def for_ahead(k):
        at = (size - k) % size
        return partial[at * rows : (at + 1) * rows].astype(F32)

    down = up = None
    for step in range(1, size):
        send_down, send_up = for_ahead(step), for_ahead(size - step)
        if step > 1:
            send_down, send_up = send_down + down.astype(F32), send_up + up.astype(F32)
        down = lax.ppermute(
            send_down.astype(BF16), "tensor", [(i, i - 1) for i in range(size - step, size)]
        )
        up = lax.ppermute(send_up.astype(BF16), "tensor", [(i, i + 1) for i in range(step)])
    return for_ahead(0) + down.astype(F32) + up.astype(F32)


class Groups:
    def __init__(self):
        self.size = lax.axis_size("dp")
        self.bits = self.size.bit_length() - 1
        me = lax.axis_index("dp")
        self.side = [(me >> b) & 1 for b in range(self.bits)]

    def swap(self, value, bit):
        return lax.ppermute(value, "dp", [(i, i ^ (1 << bit)) for i in range(self.size)])

    def halves(self, value, bit):
        half = value.shape[0] // 2
        keep = lax.dynamic_slice_in_dim(value, self.side[bit] * half, half, 0)
        give = lax.dynamic_slice_in_dim(value, (1 - self.side[bit]) * half, half, 0)
        return keep, give

    def join(self, mine, theirs, bit):
        first = self.side[bit] == 0
        return jnp.concatenate(
            [jnp.where(first, mine, theirs), jnp.where(first, theirs, mine)], axis=0
        )

    def reduce(self, value, order):
        for bit in order:
            keep, give = self.halves(value, bit)
            value = (keep.astype(F32) + self.swap(give, bit).astype(F32)).astype(BF16)
        return value

    def gather(self, value, order):
        for bit in reversed(order):
            value = self.join(value, self.swap(value, bit), bit)
        return value

    def weight_grad(self, left, right):
        half = left.shape[1] // 2
        mine = lax.dynamic_slice_in_dim(left, self.side[0] * half, half, 1)
        other = lax.dynamic_slice_in_dim(left, (1 - self.side[0]) * half, half, 1)
        came = self.swap(dot_tn(other, right).astype(BF16), 0)
        both = (dot_tn(mine, right) + came.astype(F32)).astype(BF16)
        order = list(range(1, self.bits))
        other_order = order[1:] + order[:1]
        part_a, part_b = both[: half // 2], both[half // 2 :]
        done_a, done_b = self.reduce(part_a, order), self.reduce(part_b, other_order)
        done = jnp.concatenate(
            [self.gather(done_a, order), self.gather(done_b, other_order)], axis=0
        )
        return self.join(done, self.swap(done, 0), 0).astype(F32)

    def small_sum(self, value):
        for bit in range(self.bits):
            value = value + self.swap(value, bit)
        return value


def line_sum(value, size):
    reach = 1
    while reach < size:
        value = value + lax.ppermute(value, "tensor", [(i, i ^ reach) for i in range(size)])
        reach *= 2
    return value


def shards(
    tokens,
    lengths,
    qkv_weight,
    qkv_bias,
    dense_weight,
    dense_bias,
    up_weight,
    up_bias,
    down_weight,
    down_bias,
    gain_attn,
    shift_attn,
    gain_mlp,
    shift_mlp,
    out_grad,
):
    size = lax.axis_size("tensor")
    group_size = tokens.shape[0] * size
    place = lax.axis_index("tensor").astype(jnp.int32)[None]
    groups = Groups()
    gains = (gain_attn.astype(F32), gain_mlp.astype(F32))
    shifts = (shift_attn.astype(F32), shift_mlp.astype(F32))
    first_row, position = layout(lengths[0], group_size)
    tables = rotary_tables(position)

    rows = jnp.concatenate(line_gather(tokens, size), axis=0)
    grad_all = jnp.concatenate(line_gather(after(out_grad, rows), size), axis=0)

    scaled, inverse = standardize(rows.astype(F32))
    normed_attn = (scaled * gains[0] + shifts[0]).astype(BF16)
    normed_mlp = (scaled * gains[1] + shifts[1]).astype(BF16)
    hidden = dot_nn(normed_mlp, up_weight) + up_bias.astype(F32)
    below = 0.5 * (1.0 + lax.erf(hidden * 0.5**0.5))
    active = (hidden * below).astype(BF16)
    slope = below + hidden * jnp.exp(-0.5 * hidden * hidden) * (2.0 * jnp.pi) ** -0.5
    mixed = dot_nn(normed_attn, qkv_weight) + qkv_bias.astype(F32)
    qkv, context = attend(mixed, tables, first_row, place, size)
    partial = (dot_nn(context, dense_weight) + dot_nn(active, down_weight)).astype(BF16)
    branches = line_scatter(partial, size)
    tokens_own = tokens.astype(F32)
    output = (
        tokens_own + branches + dense_bias.astype(F32) + down_bias.astype(F32)
    ).astype(BF16)

    grad_rows = out_grad.astype(F32)
    bias_part = jnp.sum(grad_rows, axis=0)
    grad_down_weight = groups.weight_grad(active, grad_all)
    grad_hidden = (dot_nt(grad_all, down_weight) * slope).astype(BF16)
    up_bias_part = jnp.sum(grad_hidden, axis=0, dtype=F32)
    grad_up_weight = groups.weight_grad(normed_mlp, grad_hidden)
    grad_context = dot_nt(grad_all, dense_weight).astype(BF16)
    grad_dense_weight = groups.weight_grad(context, grad_all)
    grad_mixed, qkv_bias_part = attend_back(qkv, grad_context, tables, first_row, place, size)
    grad_qkv_weight = groups.weight_grad(normed_attn, grad_mixed)
    mlp_grad = dot_nt(grad_hidden, up_weight)
    attn_grad = dot_nt(grad_mixed, qkv_weight)
    inner = (mlp_grad * gains[1] + attn_grad * gains[0]).astype(BF16)
    inner_own = line_scatter(inner, size)
    scaled_own, inverse_own = standardize(tokens_own)
    grad_tokens = grad_rows + inverse_own * (
        inner_own
        - jnp.mean(inner_own, axis=1, keepdims=True)
        - scaled_own * jnp.mean(inner_own * scaled_own, axis=1, keepdims=True)
    )

    width = tokens.shape[1]
    shared = groups.small_sum(
        jnp.concatenate(
            [
                jnp.sum(attn_grad * scaled, axis=0),
                jnp.sum(attn_grad, axis=0),
                jnp.sum(mlp_grad * scaled, axis=0),
                jnp.sum(mlp_grad, axis=0),
                bias_part,
                up_bias_part,
                qkv_bias_part,
            ]
        )
    )
    split = 5 * width
    everywhere = line_sum(shared[:split], size)
    gain_attn_sum, shift_attn_sum, gain_mlp_sum, shift_mlp_sum, bias_sum = (
        everywhere[k * width : (k + 1) * width] for k in range(5)
    )
    grad_up_bias = shared[split : split + up_bias.shape[0]]
    grad_qkv_bias = shared[split + up_bias.shape[0] :]
    return (
        output,
        grad_tokens,
        grad_qkv_weight,
        grad_qkv_bias,
        grad_dense_weight,
        bias_sum,
        grad_up_weight,
        grad_up_bias,
        grad_down_weight,
        bias_sum,
        gain_attn_sum,
        shift_attn_sum,
        gain_mlp_sum,
        shift_mlp_sum,
    )


def solution(mesh):
    rows = P(("dp", "tensor"), None)
    columns = P(None, "tensor")
    return jax.shard_map(
        shards,
        mesh=mesh,
        in_specs=(
            rows,
            P("dp", None),
            columns,
            P("tensor"),
            P("tensor", None),
            P(),
            columns,
            P("tensor"),
            P("tensor", None),
            P(),
            P(),
            P(),
            P(),
            P(),
            rows,
        ),
        out_specs=(
            rows,
            rows,
            columns,
            P("tensor"),
            P("tensor", None),
            P(),
            columns,
            P("tensor"),
            P("tensor", None),
            P(),
            P(),
            P(),
            P(),
            P(),
        ),
        check_vma=False,
    )
```

```python
import jax
import jax.numpy as jnp
from jax import lax
from jax.experimental import pallas as pl
from jax.experimental.pallas import tpu as pltpu
from jax.sharding import PartitionSpec as P

HEAD_DIM = 128
ROT = 32
EPSILON = 1e-05
MASKED = -1e30
BF16 = jnp.bfloat16
F32 = jnp.float32


def standardize(row_block):
    average = jnp.mean(row_block, axis=1, keepdims=True)
    centred = row_block - average
    inverse = lax.rsqrt(jnp.mean(centred * centred, axis=1, keepdims=True) + EPSILON)
    return (centred * inverse, inverse)


def layout(lengths, group_size):
    seq_ends = jnp.cumsum(lengths)
    row_ids = jnp.arange(group_size, dtype=jnp.int32)
    passed = (seq_ends[None, :] <= row_ids[:, None]).astype(jnp.int32)
    first_row = jnp.sum(passed * lengths[None, :], axis=1)
    return (first_row, row_ids - first_row)


def rotary_tables(position):
    exponents = jnp.arange(0, ROT, 2, dtype=F32) / ROT
    inv_freq = 1.0 / 10000.0**exponents
    angles = position.astype(F32)[:, None] * inv_freq[None, :]
    cosine, sine = jnp.cos(angles), jnp.sin(angles)
    rows, half = angles.shape
    keep = jnp.concatenate([cosine, cosine, jnp.ones((rows, HEAD_DIM - ROT), F32)], axis=1)
    low = jnp.concatenate([-sine, jnp.zeros((rows, HEAD_DIM - half), F32)], axis=1)
    high = jnp.concatenate(
        [jnp.zeros((rows, half), F32), sine, jnp.zeros((rows, HEAD_DIM - ROT), F32)], axis=1
    )
    return (keep, low, high)


def turn(u, keep, low, high):
    return (
        u * keep
        + pltpu.roll(u, HEAD_DIM - ROT // 2, 1) * low
        + pltpu.roll(u, ROT // 2, 1) * high
    )


def turn_back(u, keep, low, high):
    return (
        u * keep
        - pltpu.roll(u, HEAD_DIM - ROT // 2, 1) * low
        - pltpu.roll(u, ROT // 2, 1) * high
    )


def dot_nt(a, b):
    return lax.dot_general(a, b, (((1,), (1,)), ((), ())), preferred_element_type=F32)


def dot_tn(a, b):
    return lax.dot_general(a, b, (((0,), (0,)), ((), ())), preferred_element_type=F32)


def dot_nn(a, b):
    return jnp.dot(a, b, preferred_element_type=F32)


def attend_kernel(blocks, mixed_ref, keep_ref, low_ref, high_ref, first_ref, qkv_ref, context_ref):
    rows = mixed_ref.shape[0] // blocks
    scale = HEAD_DIM ** (-0.5)

    def slot(i):
        return slice(i * rows, (i + 1) * rows)

    for i in range(blocks):
        here = slice(i * rows, (i + 1) * rows)
        tables = (keep_ref[here, :], low_ref[here, :], high_ref[here, :])
        there = slot(i)
        qkv_ref[here, 0:128] = turn(mixed_ref[there, 0:128], *tables).astype(BF16)
        qkv_ref[here, 128:256] = turn(mixed_ref[there, 128:256], *tables).astype(BF16)
        qkv_ref[here, 256:384] = mixed_ref[there, 256:384].astype(BF16)
    for i in range(blocks):
        count = (i + 1) * rows
        query = qkv_ref[i * rows : count, 0:128]
        scores = dot_nt(query, qkv_ref[0:count, 128:256]) * scale
        key_at = lax.broadcasted_iota(jnp.int32, scores.shape, 1)
        query_at = lax.broadcasted_iota(jnp.int32, scores.shape, 0) + i * rows
        seen = (key_at >= first_ref[i * rows : count, :]) & (key_at <= query_at)
        scores = jnp.where(seen, scores, MASKED)
        top = jnp.max(scores, axis=1, keepdims=True)
        raised = jnp.exp(scores - top)
        total = jnp.sum(raised, axis=1, keepdims=True)
        weights = (raised * (1.0 / total)).astype(BF16)
        context_ref[slot(i), :] = dot_nn(weights, qkv_ref[0:count, 256:384]).astype(BF16)


def attend(mixed, tables, first_row, blocks):
    group, width = mixed.shape
    heads = width // (3 * HEAD_DIM)
    whole = lambda h: (0, 0)
    by_head = lambda h: (0, h)
    table = pl.BlockSpec((group, HEAD_DIM), whole)
    return pl.pallas_call(
        lambda *refs: attend_kernel(blocks, *refs),
        out_shape=(
            jax.ShapeDtypeStruct((group, width), BF16),
            jax.ShapeDtypeStruct((group, heads * HEAD_DIM), BF16),
        ),
        grid_spec=pltpu.PrefetchScalarGridSpec(
            num_scalar_prefetch=0,
            grid=(heads,),
            in_specs=[
                pl.BlockSpec((group, 3 * HEAD_DIM), by_head),
                table,
                table,
                table,
                pl.BlockSpec((group, 1), whole),
            ],
            out_specs=(
                pl.BlockSpec((group, 3 * HEAD_DIM), by_head),
                pl.BlockSpec((group, HEAD_DIM), by_head),
            ),
        ),
        compiler_params=pltpu.CompilerParams(dimension_semantics=("arbitrary",)),
        name="attend",
    )(mixed, *tables, first_row[:, None])


def attend_back_kernel(
    blocks,
    qkv_ref,
    grad_ref,
    keep_ref,
    low_ref,
    high_ref,
    first_ref,
    mixed_ref,
    sums_ref,
    keys_ref,
    values_ref,
):
    rows = qkv_ref.shape[0] // blocks
    scale = HEAD_DIM ** (-0.5)

    def slot(i):
        return slice(i * rows, (i + 1) * rows)

    def tables(i):
        here = slice(i * rows, (i + 1) * rows)
        return (keep_ref[here, :], low_ref[here, :], high_ref[here, :])

    query_sum = jnp.zeros((1, HEAD_DIM), F32)
    key_sum = jnp.zeros((1, HEAD_DIM), F32)
    value_sum = jnp.zeros((1, HEAD_DIM), F32)
    for i in reversed(range(blocks)):
        count = (i + 1) * rows
        query = qkv_ref[i * rows : count, 0:128]
        keys = qkv_ref[0:count, 128:256]
        grad = grad_ref[slot(i), :]
        scores = dot_nt(keys, query) * scale
        key_at = lax.broadcasted_iota(jnp.int32, scores.shape, 0)
        query_at = lax.broadcasted_iota(jnp.int32, scores.shape, 1) + i * rows
        seen = (key_at >= first_ref[:, i * rows : count]) & (key_at <= query_at)
        scores = jnp.where(seen, scores, MASKED)
        top = jnp.max(scores, axis=0, keepdims=True)
        raised = jnp.exp(scores - top)
        total = jnp.sum(raised, axis=0, keepdims=True)
        probs = raised * (1.0 / total)
        grad_values = dot_nn(probs.astype(BF16), grad)
        grad_probs = dot_nt(qkv_ref[0:count, 256:384], grad)
        spread = jnp.sum(probs * grad_probs, axis=0, keepdims=True)
        grad_scores = (probs * (grad_probs - spread)).astype(BF16)
        grad_keys = dot_nn(grad_scores, query)
        if i == blocks - 1:
            values_ref[...] = grad_values
            keys_ref[...] = grad_keys
        else:
            values_ref[0:count, :] += grad_values
            keys_ref[0:count, :] += grad_keys
        grad_query = turn_back(dot_tn(grad_scores, keys) * scale, *tables(i)).astype(BF16)
        mixed_ref[slot(i), 0:128] = grad_query
        query_sum += jnp.sum(grad_query.astype(F32), axis=0, keepdims=True)
        here = slice(i * rows, count)
        if i == 0:
            for j in range(blocks):
                here = slice(j * rows, (j + 1) * rows)
                grad_key = turn_back(keys_ref[here, :] * scale, *tables(j)).astype(BF16)
                grad_value = values_ref[here, :].astype(BF16)
                mixed_ref[slot(j), 128:256] = grad_key
                mixed_ref[slot(j), 256:384] = grad_value
                key_sum += jnp.sum(grad_key.astype(F32), axis=0, keepdims=True)
                value_sum += jnp.sum(grad_value.astype(F32), axis=0, keepdims=True)
    sums_ref[:, 0:128] = jnp.broadcast_to(query_sum, (8, HEAD_DIM))
    sums_ref[:, 128:256] = jnp.broadcast_to(key_sum, (8, HEAD_DIM))
    sums_ref[:, 256:384] = jnp.broadcast_to(value_sum, (8, HEAD_DIM))


def attend_back(qkv, grad_context, tables, first_row, blocks):
    group, width = qkv.shape
    heads = width // (3 * HEAD_DIM)
    whole = lambda h: (0, 0)
    by_head = lambda h: (0, h)
    table = pl.BlockSpec((group, HEAD_DIM), whole)
    mixed, sums = pl.pallas_call(
        lambda *refs: attend_back_kernel(blocks, *refs),
        out_shape=(
            jax.ShapeDtypeStruct((group, width), BF16),
            jax.ShapeDtypeStruct((8, width), F32),
        ),
        grid_spec=pltpu.PrefetchScalarGridSpec(
            num_scalar_prefetch=0,
            grid=(heads,),
            in_specs=[
                pl.BlockSpec((group, 3 * HEAD_DIM), by_head),
                pl.BlockSpec((group, HEAD_DIM), by_head),
                table,
                table,
                table,
                pl.BlockSpec((1, group), whole),
            ],
            out_specs=(
                pl.BlockSpec((group, 3 * HEAD_DIM), by_head),
                pl.BlockSpec((8, 3 * HEAD_DIM), by_head),
            ),
            scratch_shapes=[pltpu.VMEM((group, HEAD_DIM), F32)] * 2,
        ),
        compiler_params=pltpu.CompilerParams(dimension_semantics=("arbitrary",)),
        name="attend_back",
    )(qkv, grad_context, *tables, first_row[None, :])
    return (mixed, sums[0])


def forward_kernel(
    up_steps,
    rows_ref,
    gain_attn_ref,
    shift_attn_ref,
    gain_mlp_ref,
    shift_mlp_ref,
    up_ref,
    up_bias_ref,
    qkv_ref,
    qkv_bias_ref,
    *refs,
):
    outs = refs[-9:]
    all_ref, attn_ref, mlp_ref, mean_ref, inverse_ref, active_ref, slope_ref, mixed_ref = outs[:8]
    scratch_ref = outs[8]
    devices, _, rows, width = attn_ref.shape
    at = pl.program_id(0)

    @pl.when(at == 0)
    def _():
        for d in range(devices):
            here = slice(d * rows, (d + 1) * rows)
            piece = rows_ref[here, :]
            values = piece.astype(F32)
            average = jnp.mean(values, axis=1, keepdims=True)
            centred = values - average
            inverse = lax.rsqrt(jnp.mean(centred * centred, axis=1, keepdims=True) + EPSILON)
            scaled = centred * inverse
            attn = (scaled * gain_attn_ref[...] + shift_attn_ref[...]).astype(BF16)
            mlp = (scaled * gain_mlp_ref[...] + shift_mlp_ref[...]).astype(BF16)
            all_ref[d, 0] = piece
            attn_ref[d, 0] = attn
            mlp_ref[d, 0] = mlp
            mean_ref[d, 0] = average
            inverse_ref[d, 0] = inverse
            scratch_ref[0, here, :] = mlp
            scratch_ref[1, here, :] = attn

    @pl.when(at < up_steps)
    def _():
        for d in range(devices):
            here = slice(d * rows, (d + 1) * rows)
            hidden = dot_nn(scratch_ref[0, here, :], up_ref[...]) + up_bias_ref[...]
            below = 0.5 * (1.0 + lax.erf(hidden * 0.5**0.5))
            bell = jnp.exp(-0.5 * hidden * hidden) * (2.0 * jnp.pi) ** -0.5
            active_ref[d, 0] = (hidden * below).astype(BF16)
            slope_ref[d, 0] = (below + hidden * bell).astype(BF16)

    @pl.when(at >= up_steps)
    def _():
        for d in range(devices):
            here = slice(d * rows, (d + 1) * rows)
            mixed_ref[d, 0] = dot_nn(scratch_ref[1, here, :], qkv_ref[...]) + qkv_bias_ref[...]


def forward(gathered, part, vectors, up_weight, up_bias, qkv_weight, qkv_bias, devices, buffers):
    count, width = gathered.shape
    rows = count // devices
    hidden, third = up_weight.shape[1], qkv_weight.shape[1]
    up_part, qkv_part = hidden // 4, third // 3
    up_steps, steps = 4, 7
    up_at = lambda j: jnp.minimum(j, up_steps - 1)
    qkv_at = lambda j: jnp.maximum(j - up_steps, 0)
    vector = pl.BlockSpec((1, width), lambda j: (0, 0))
    whole = lambda n: pl.BlockSpec((devices, 1, rows, n), lambda j: (0, part, 0, 0))
    up_out = pl.BlockSpec((devices, 1, rows, up_part), lambda j: (0, part, 0, up_at(j)))
    shape = lambda n, t: jax.ShapeDtypeStruct((devices, 2, rows, n), t)
    return pl.pallas_call(
        lambda *refs: forward_kernel(up_steps, *refs),
        out_shape=[
            shape(width, BF16),
            shape(width, BF16),
            shape(width, BF16),
            shape(1, F32),
            shape(1, F32),
            shape(hidden, BF16),
            shape(hidden, BF16),
            shape(third, F32),
        ],
        grid=(steps,),
        in_specs=[pl.BlockSpec((count, width), lambda j: (0, 0))]
        + [vector] * 4
        + [
            pl.BlockSpec((width, up_part), lambda j: (0, up_at(j))),
            pl.BlockSpec((1, up_part), lambda j: (0, up_at(j))),
            pl.BlockSpec((width, qkv_part), lambda j: (0, qkv_at(j))),
            pl.BlockSpec((1, qkv_part), lambda j: (0, qkv_at(j))),
        ]
        + [pl.BlockSpec(memory_space=pl.ANY)] * len(buffers),
        out_specs=[
            whole(width),
            whole(width),
            whole(width),
            whole(1),
            whole(1),
            up_out,
            up_out,
            pl.BlockSpec((devices, 1, rows, qkv_part), lambda j: (0, part, 0, qkv_at(j))),
        ],
        scratch_shapes=[pltpu.VMEM((2, count, width), BF16)],
        input_output_aliases={9 + k: k for k in range(len(buffers))},
        name="forward",
    )(
        gathered,
        *vectors,
        up_weight,
        up_bias.astype(F32)[None, :],
        qkv_weight,
        qkv_bias.astype(F32)[None, :],
        *buffers,
    )


def hidden_back_kernel(sloped, one_ref, two_ref, weight_ref, *refs):
    group, half = one_ref.shape
    grad_ref = refs[1] if sloped else refs[0]
    step = min(group, 256)
    sums = jnp.zeros((1, grad_ref.shape[1]), F32)
    for r in range(0, group, step):
        here = slice(r, r + step)
        grad = dot_nt(one_ref[here, :], weight_ref[:, :half])
        grad += dot_nt(two_ref[here, :], weight_ref[:, half:])
        if sloped:
            grad = grad * refs[0][here, :].astype(F32)
        grad = grad.astype(BF16)
        grad_ref[here, :] = grad
        if sloped:
            sums += jnp.sum(grad.astype(F32), axis=0, keepdims=True)
    if sloped:
        refs[2][...] = jnp.broadcast_to(sums, refs[2].shape)


def hidden_back(one, two, weight, slope=None):
    group, half = one.shape
    hidden = weight.shape[0]
    sloped = slope is not None
    part = min(hidden, 512 if sloped else 256)
    kept = pl.BlockSpec((group, half), lambda j: (0, 0), pipeline_mode=pl.Buffered(1))
    columns = pl.BlockSpec((group, part), lambda j: (0, j))
    out = [jax.ShapeDtypeStruct((group, hidden), BF16), jax.ShapeDtypeStruct((8, hidden), F32)]
    specs = [columns, pl.BlockSpec((8, part), lambda j: (0, j))]
    count = 2 if sloped else 1
    return pl.pallas_call(
        lambda *refs: hidden_back_kernel(sloped, *refs),
        out_shape=out[:count],
        grid=(hidden // part,),
        in_specs=[kept, kept, pl.BlockSpec((part, 2 * half), lambda j: (j, 0))]
        + ([columns] if sloped else []),
        out_specs=specs[:count],
        name="hidden_back" if sloped else "context_back",
    )(one, two, weight, *((slope,) if sloped else ()))


def inner_kernel(
    hidden_ref,
    up_ref,
    mixed_ref,
    qkv_ref,
    rows_ref,
    mean_ref,
    inverse_ref,
    gain_attn_ref,
    gain_mlp_ref,
    inner_ref,
    sums_ref,
):
    group, width = inner_ref.shape
    step = min(group, 256)
    totals = [jnp.zeros((1, width), F32) for _ in range(4)]
    for r in range(0, group, step):
        here = slice(r, r + step)
        mlp = dot_nt(hidden_ref[here, :], up_ref[...])
        attn = dot_nt(mixed_ref[here, :], qkv_ref[...])
        scaled = (rows_ref[here, :].astype(F32) - mean_ref[here, :]) * inverse_ref[here, :]
        inner_ref[here, :] = (mlp * gain_mlp_ref[...] + attn * gain_attn_ref[...]).astype(BF16)
        for k, term in enumerate((attn * scaled, attn, mlp * scaled, mlp)):
            totals[k] += jnp.sum(term, axis=0, keepdims=True)
    for k in range(4):
        sums_ref[k : k + 1, :] = totals[k]


def inner_grad(grad_hidden, up_weight, grad_mixed, qkv_weight, rows, mean, inverse, gains):
    group, hidden = grad_hidden.shape
    third = grad_mixed.shape[1]
    width = rows.shape[1]
    part = min(width, 512)
    once = pl.Buffered(1)
    row = pl.BlockSpec((1, part), lambda j: (0, j))
    columns = pl.BlockSpec((group, part), lambda j: (0, j))
    column = pl.BlockSpec((group, 1), lambda j: (0, 0))
    return pl.pallas_call(
        inner_kernel,
        out_shape=(
            jax.ShapeDtypeStruct((group, width), BF16),
            jax.ShapeDtypeStruct((4, width), F32),
        ),
        grid=(width // part,),
        in_specs=[
            pl.BlockSpec((group, hidden), lambda j: (0, 0), pipeline_mode=once),
            pl.BlockSpec((part, hidden), lambda j: (j, 0)),
            pl.BlockSpec((group, third), lambda j: (0, 0), pipeline_mode=once),
            pl.BlockSpec((part, third), lambda j: (j, 0)),
            columns,
            column,
            column,
            row,
            row,
        ],
        out_specs=(columns, pl.BlockSpec((4, part), lambda j: (0, j))),
        name="inner_grad",
    )(grad_hidden, up_weight, grad_mixed, qkv_weight, rows, mean, inverse, *gains)


def widen_kernel(rows, offset, column, sides_ref, *refs):
    pieces, out_ref = refs[:8], refs[-5]
    came, wide, came_sems, wide_sems = refs[-4:]
    width = wide.shape[2]

    def bring(k):
        source = pieces[k].at[offset : offset + rows, :]
        return pltpu.make_async_copy(source, came.at[k], came_sems.at[k])

    def send(k):
        at = (((k >> 2) ^ sides_ref[0]) << 2) + (k & 2) + ((k & 1) ^ sides_ref[1 + ((k >> 1) & 1)])
        target = out_ref.at[
            pl.ds(pl.multiple_of(at * rows, rows), rows), column * width : (column + 1) * width
        ]
        return pltpu.make_async_copy(wide.at[k & 1], target, wide_sems.at[k])

    for k in range(8):
        bring(k).start()
    for k in range(8):
        bring(k).wait()
        if k > 1:
            send(k - 2).wait()
        wide[k & 1] = came[k].astype(F32)
        send(k).start()
    send(6).wait()
    send(7).wait()


def widen(pieces, sides, rows, offset, full, column, buffers):
    width = pieces[0].shape[1]
    anywhere = pl.BlockSpec(memory_space=pl.ANY)
    return pl.pallas_call(
        lambda *refs: widen_kernel(rows, offset, column, *refs),
        out_shape=jax.ShapeDtypeStruct(full, F32),
        grid_spec=pltpu.PrefetchScalarGridSpec(
            num_scalar_prefetch=1,
            grid=(),
            in_specs=[anywhere] * (8 + len(buffers)),
            out_specs=anywhere,
            scratch_shapes=[
                pltpu.VMEM((8, rows, width), BF16),
                pltpu.VMEM((2, rows, width), F32),
                pltpu.SemaphoreType.DMA((8,)),
                pltpu.SemaphoreType.DMA((8,)),
            ],
        ),
        input_output_aliases={9: 0} if buffers else {},
        name="widen",
    )(sides, *pieces, *buffers)


def after(value, *earlier):
    return lax.optimization_barrier((value, *earlier))[0]


class Order:
    def __init__(self):
        self.last = ()

    def __call__(self, work, *inputs):
        inputs, _ = lax.optimization_barrier((inputs, self.last))
        result = work(*inputs)
        self.last = result
        return result

    def wait(self, *values):
        self.last = (self.last, values)


class Groups:
    def __init__(self):
        self.size = lax.axis_size("dp")
        self.bits = self.size.bit_length() - 1
        me = lax.axis_index("dp")
        self.side = [(me >> b) & 1 for b in range(self.bits)]
        self.order_a = list(range(1, self.bits))
        self.order_b = self.order_a[1:] + self.order_a[:1]
        self.sides = jnp.stack(
            [self.side[0], self.side[self.order_a[0]], self.side[self.order_b[0]]]
        ).astype(jnp.int32)

    def swap(self, value, bit):
        return lax.ppermute(value, "dp", [(i, i ^ (1 << bit)) for i in range(self.size)])

    def half(self, value, bit, own, axis=0):
        half = value.shape[axis] // 2
        side = self.side[bit] if own else 1 - self.side[bit]
        return lax.dynamic_slice_in_dim(value, side * half, half, axis)

    def join(self, mine, theirs, bit):
        first = self.side[bit] == 0
        return jnp.concatenate(
            [jnp.where(first, mine, theirs), jnp.where(first, theirs, mine)], axis=0
        )

    def chunk(self, run, lefts, right):
        sizes = [left.shape[1] for left in lefts]

        def product(own, *came):
            def work(right, *values):
                out = []
                for k in range(len(lefts)):
                    value = dot_tn(self.half(values[k], 0, own, 1), right)
                    if own:
                        value = value + values[len(lefts) + k].astype(F32)
                    out.append(value.astype(BF16))
                return tuple(out)

            return run(work, right, *lefts, *came)

        came = tuple(self.swap(value, 0) for value in product(False))
        yield None
        both = product(True, *came)

        def split(both):
            branch = lambda b: [
                p[: p.shape[0] // 2] if b == 0 else p[p.shape[0] // 2 :] for p in both
            ]
            return [branch(0), branch(1)]

        def rows_of(parts):
            return parts[0] if len(parts) == 1 else jnp.concatenate(parts, axis=0)

        def cut(value, like):
            out, start = [], 0
            for n in like:
                out.append(value[start : start + n])
                start += n
            return out

        orders = (self.order_a, self.order_b)
        counts = [n // 4 for n in sizes]

        def first_gives(*both):
            branches = split(both)
            return tuple(
                rows_of([self.half(p, orders[b][0], False) for p in branches[b]]) for b in (0, 1)
            )

        def first_keeps(*both):
            branches = split(both)
            return tuple(
                rows_of([self.half(p, orders[b][0], True) for p in branches[b]]) for b in (0, 1)
            )

        gives = run(first_gives, *both)
        keeps = None
        for step in range(self.bits - 1):
            got = tuple(self.swap(gives[b], orders[b][step]) for b in (0, 1))
            yield None
            counts = [n // 2 for n in counts]
            first, last = step == 0, step == self.bits - 2

            def add(*values):
                *kept, got_a, got_b = values
                kept = first_keeps(*kept) if first else kept
                sums = [
                    (k.astype(F32) + g.astype(F32)).astype(BF16)
                    for k, g in zip(kept, (got_a, got_b))
                ]
                if last:
                    return tuple(sums)
                parts = [cut(s, counts) for s in sums]
                pick = lambda own: tuple(
                    rows_of([self.half(p, orders[b][step + 1], own) for p in parts[b]])
                    for b in (0, 1)
                )
                return pick(False) + pick(True)

            out = run(add, *(both if first else keeps), *got)
            gives, keeps = out[:2], out[2:]
        done = gives
        for step in reversed(range(1, self.bits - 1)):
            got = tuple(self.swap(done[b], orders[b][step]) for b in (0, 1))
            yield None

            def joins(*values):
                out = []
                for b in (0, 1):
                    mine, theirs = cut(values[b], counts), cut(values[2 + b], counts)
                    out.append(
                        rows_of(
                            [self.join(m, t, orders[b][step]) for m, t in zip(mine, theirs)]
                        )
                    )
                return tuple(out)

            done = run(joins, *done, *got)
            counts = [n * 2 for n in counts]
        got = tuple(self.swap(done[b], orders[b][0]) for b in (0, 1))
        near = tuple(self.swap(done[b], 0) for b in (0, 1))
        yield None
        run.wait(*got)
        far = tuple(self.swap(got[b], 0) for b in (0, 1))
        yield ((done[0], got[0], done[1], got[1], near[0], far[0], near[1], far[1]), counts)


def small_sum(run, groups, shared, split, size):
    add = lambda a, b: a + b
    for bit in range(groups.bits):
        got = groups.swap(shared, bit)
        yield None
        shared = run(add, shared, got)
    everywhere = shared[:, :split]
    reach = 1
    while reach < size:
        got = lax.ppermute(everywhere, "tensor", [(i, i ^ reach) for i in range(size)])
        yield None
        everywhere = run(add, everywhere, got)
        reach *= 2
    yield everywhere[0], shared[0, split:]


def shards(
    tokens,
    lengths,
    qkv_weight,
    qkv_bias,
    dense_weight,
    dense_bias,
    up_weight,
    up_bias,
    down_weight,
    down_bias,
    gain_attn,
    shift_attn,
    gain_mlp,
    shift_mlp,
    out_grad,
):
    size = lax.axis_size("tensor")
    width = tokens.shape[1]
    own_rows = tokens.shape[0]
    group_size = own_rows * size
    blocks = max(group_size // 256, 1)
    groups = Groups()
    run = Order()
    half = width // 2

    top = lax.all_gather(tokens[: own_rows // 2], "tensor", axis=0, tiled=True)
    bottom = lax.all_gather(after(tokens[own_rows // 2 :], top), "tensor", axis=0, tiled=True)
    grad_one = lax.all_gather(after(out_grad[:, :half], bottom), "tensor", axis=0, tiled=True)
    grad_two = lax.all_gather(after(out_grad[:, half:], grad_one), "tensor", axis=0, tiled=True)

    first_row, position = layout(lengths[0], group_size)
    tables = rotary_tables(position)
    vectors = [v.astype(F32)[None, :] for v in (gain_attn, shift_attn, gain_mlp, shift_mlp)]
    tokens_own = tokens.astype(F32)
    grad_rows = out_grad.astype(F32)
    bias_part = jnp.sum(grad_rows, axis=0)

    buffers = ()
    for part, gathered in enumerate((top, bottom)):
        buffers = run(
            lambda g, *b: forward(
                g, part, vectors, up_weight, up_bias, qkv_weight, qkv_bias, size, b
            ),
            gathered,
            *buffers,
        )
    rows, normed_attn, normed_mlp, mean, inverse, active, slope, mixed = (
        b.reshape(group_size, b.shape[3]) for b in buffers
    )
    qkv, context = run(lambda m: attend(m, tables, first_row, blocks), mixed)
    down_one = groups.chunk(run, [active, context], grad_one)
    next(down_one)
    next(down_one)
    partial = run(
        lambda c, a: (dot_nn(c, dense_weight) + dot_nn(a, down_weight)).astype(BF16),
        context,
        active,
    )
    branches = lax.psum_scatter(
        after(partial, grad_two), "tensor", scatter_dimension=0, tiled=True
    )
    next(down_one)
    next(down_one)
    down_two = groups.chunk(run, [active, context], grad_two)
    next(down_two)
    next(down_one)
    next(down_two)
    grad_hidden, up_bias_part = run(
        lambda a, b: hidden_back(a, b, down_weight, slope), grad_one, grad_two
    )
    pieces_one, counts = final(down_one)
    up = groups.chunk(run, [normed_mlp], grad_hidden)
    next(up)
    next(down_two)
    next(up)
    (grad_context,) = run(lambda a, b: hidden_back(a, b, dense_weight), grad_one, grad_two)
    next(down_two)
    grad_mixed, qkv_bias_part = run(
        lambda q, g: attend_back(q, g, tables, first_row, blocks), qkv, grad_context
    )
    next(down_two)
    next(up)
    inner, sums = run(
        lambda h, m: inner_grad(
            h, up_weight, m, qkv_weight, rows, mean, inverse, (vectors[0], vectors[2])
        ),
        grad_hidden,
        grad_mixed,
    )
    inner_own = lax.psum_scatter(inner, "tensor", scatter_dimension=0, tiled=True)
    pieces_two, counts = final(down_two)
    next(up)
    last = groups.chunk(run, [normed_attn], grad_mixed)
    next(last)
    next(last)
    next(up)
    split = 5 * width
    shared = jnp.concatenate([sums.reshape(-1), bias_part, up_bias_part[0], qkv_bias_part])
    totals = small_sum(run, groups, shared[None, :], split, size)
    full_down, full_dense = down_weight.shape, dense_weight.shape
    grad_down = run(
        lambda *p: widen(p, groups.sides, counts[0], 0, full_down, 0, ()), *pieces_one
    )
    next(totals)
    grad_dense = run(
        lambda *p: widen(p, groups.sides, counts[1], counts[0], full_dense, 0, ()), *pieces_one
    )
    next(totals)
    grad_down = run(
        lambda b, *p: widen(p, groups.sides, counts[0], 0, full_down, 1, (b,)),
        grad_down,
        *pieces_two,
    )
    next(last)
    next(totals)
    grad_dense = run(
        lambda b, *p: widen(p, groups.sides, counts[1], counts[0], full_dense, 1, (b,)),
        grad_dense,
        *pieces_two,
    )
    output = run(
        lambda b: (
            tokens.astype(F32) + b.astype(F32) + dense_bias.astype(F32) + down_bias.astype(F32)
        ).astype(BF16),
        branches,
    )
    next(last)
    pieces_up, counts = final(up)
    next(totals)
    next(last)
    grad_up = run(
        lambda *p: widen(p, groups.sides, counts[0], 0, up_weight.shape, 0, ()), *pieces_up
    )
    next(totals)
    everywhere, here = final(totals)

    def tokens_work(inner_own):
        inner_own = inner_own.astype(F32)
        scaled_own, inverse_own = standardize(tokens_own)
        return grad_rows + inverse_own * (
            inner_own
            - jnp.mean(inner_own, axis=1, keepdims=True)
            - scaled_own * jnp.mean(inner_own * scaled_own, axis=1, keepdims=True)
        )

    pieces_last, counts = final(last)
    grad_qkv = run(
        lambda *p: widen(p, groups.sides, counts[0], 0, qkv_weight.shape, 0, ()), *pieces_last
    )
    grad_tokens = run(tokens_work, inner_own)
    gain_attn_sum, shift_attn_sum, gain_mlp_sum, shift_mlp_sum, bias_sum = (
        everywhere[k * width : (k + 1) * width] for k in range(5)
    )
    return (
        output,
        grad_tokens,
        grad_qkv,
        here[up_bias.shape[0] :],
        grad_dense,
        bias_sum,
        grad_up,
        here[: up_bias.shape[0]],
        grad_down,
        bias_sum,
        gain_attn_sum,
        shift_attn_sum,
        gain_mlp_sum,
        shift_mlp_sum,
    )


def final(stages):
    *_, result = stages
    return result


def solution(mesh):
    rows = P(("dp", "tensor"), None)
    columns = P(None, "tensor")
    return jax.shard_map(
        shards,
        mesh=mesh,
        in_specs=(
            rows,
            P("dp", None),
            columns,
            P("tensor"),
            P("tensor", None),
            P(),
            columns,
            P("tensor"),
            P("tensor", None),
            P(),
            P(),
            P(),
            P(),
            P(),
            rows,
        ),
        out_specs=(
            rows,
            rows,
            columns,
            P("tensor"),
            P("tensor", None),
            P(),
            columns,
            P("tensor"),
            P("tensor", None),
            P(),
            P(),
            P(),
            P(),
            P(),
        ),
        check_vma=False,
    )
```
